32 devices in a mesh: rows: 8 (over z, x), grp: 4 (over y, core).
Axes of the slice: x: 2, y: 2, z: 4, core: 2. Of those that a mesh axis runs over, the one named last changes fastest.
Arguments:
- bin_codes: int32 [131072, 512], P(('rows', 'grp')), may hold values from 0 to 31
- leaf_index: int32 [131072, 1], P(('rows', 'grp')), may hold values from 0 to 7; in each aligned block of 4096 rows (0 to 4095, 4096 to 8191, ...) at most 1024 rows name the same one
- gradients: bfloat16 [131072, 16], P(('rows', 'grp')), may hold values from -6 to 6
- row_weights: bfloat16 [131072], P(('rows', 'grp')), may hold values from 0.5 to 2
- split_feature: int32 [1], replicated, may hold values from 0 to 511
- split_bin: int32 [1], replicated, may hold values from 0 to 30
Outputs:
- gain_table: float32 [16384], P('rows')
- best_gain: float32 [1], replicated
- moved_gradients: bfloat16 [64, 65536], P(('rows', 'grp'))
- moved_weights: bfloat16 [64, 4096], P(('rows', 'grp'))
The draws below stay inside these ranges and needn't reach their ends.
Inputs may be any that keep to these rules, and one draw needn't show every extreme that they name: `leaf_index`: among the rows of one device, each leaf holds at most 1024 rows, and some leaf holds exactly 1024 on some devices.
All inputs are finite; a program needn't handle non-finite values.
Results may differ from the reference program's by a relative error of at most 0.0004.
Values may be sent and summed in bfloat16 or wider, within the bound.
A program may use at most 128 MiB of HBM per device.

```python
import math
import jax
import jax.numpy as jnp
import numpy as np
from jax import lax

FEATURES = 512
BINS = 32
TARGETS = 16
LEAVES = 8
ROW_DEV = 4096
CAP = 1024
TOTAL_ROWS = 131072
N_ROWS = 8
N_GRP = 4


def touch_ends(array, own_key, smallest, top_value):
    longest = array.shape.index(max(array.shape))
    spots = []
    for shift in (0, 1):
        where = [jax.random.randint(jax.random.fold_in(own_key, axis), (), 0, length) for axis, length in enumerate(array.shape)]
        where[longest] = (where[longest] + shift) % array.shape[longest]
        spots.append(tuple(where))
    return array.at[spots[0]].set(smallest).at[spots[1]].set(top_value)


def levels(stream_key, extent, pieces, low, high):
    gain, own = 1.0, jax.random.fold_in(stream_key, 6)
    for axis_at, shards_of in pieces:
        steps = jnp.exp(jax.random.uniform(jax.random.fold_in(own, axis_at), (shards_of,), jnp.float32, low / len(pieces), high / len(pieces)))
        gain = gain * jnp.repeat(steps, extent[axis_at] // shards_of).reshape([-1 if axis == axis_at else 1 for axis in range(len(extent))])
    return gain


def assign_block(stream_key, own, number, rows, amount, top, limit, slope):
    ranking = jax.random.permutation(stream_key, amount)
    crowded, usual = load_shares(amount, rows * top, limit, slope, True), load_shares(amount, rows * top, limit, slope, False)
    places = jnp.arange(amount)

    def named(sizes, turn):
        used = int((sizes > 0).sum())
        fixed = max(1, used // 4)
        passed = fixed + (places - fixed + turn * (used - fixed)) % max(1, amount - fixed)
        return jnp.zeros((amount,), jnp.int32).at[ranking[jnp.where(places < fixed, places, passed)]].set(jnp.asarray(sizes, jnp.int32))

    sizes = jnp.where(number % 4 == 0, named(crowded, number // 4), named(usual, number - number // 4 - 1))
    mixed = jax.random.permutation(jax.random.fold_in(own, 3), amount)
    donor, receiver = mixed[0:amount // 2 * 2:2], mixed[1:amount // 2 * 2:2]
    slack = jnp.minimum(sizes[donor] - 1, limit - sizes[receiver]) // 2
    slack = jnp.where((donor == ranking[0]) | (receiver == ranking[0]) | (sizes[receiver] == 0), 0, jnp.maximum(slack, 0))
    passed = jax.random.randint(jax.random.fold_in(own, 4), (amount // 2,), 0, 1 << 20) % (slack + 1)
    sizes = sizes.at[donor].add(-passed).at[receiver].add(passed)
    members = jnp.searchsorted(jnp.cumsum(sizes), jnp.arange(rows * top), side="right").astype(jnp.int32)
    listing = members.reshape(top, rows).T
    listing = listing[jax.random.permutation(jax.random.fold_in(own, 1), rows)]
    turn = jax.random.randint(jax.random.fold_in(own, 2), (rows, 1), 0, top)
    return jnp.take_along_axis(listing, (jnp.arange(top)[None, :] + turn) % top, axis=1)


def load_shares(amount, total, most, lean, full):
    weights = [(1 << 20) // math.isqrt(rank ** lean) + 1 for rank in range(1, amount + 1)]
    largest = most if full else min(most, max(-(-total // amount), total * weights[0] // sum(weights)))
    least = 1 if total - largest >= amount - 1 else 0
    given, rest = [largest] + [least] * (amount - 1), total - largest - least * (amount - 1)
    while rest > 0:
        candidates = [i for i in range(1, amount) if given[i] < largest] or [i for i in range(1, amount) if given[i] < most]
        whole, budget = sum([weights[i] for i in candidates]), rest
        for i in candidates:
            addition = min(most - given[i], max(1, budget * weights[i] // whole), rest)
            given[i] = given[i] + addition
            rest = rest - addition
    return np.array(given)


def bell_draw(stream_key, shape, scale, most, split=(), kind=jnp.bfloat16):
    array = jax.random.normal(stream_key, shape, jnp.float32) * scale
    if len(split) > 0:
        array = levels(stream_key, shape, split, -0.22, 0.18) * array
    return jnp.clip(array, min=-most, max=most).astype(kind)


def setup_inputs(seed: int = 0) -> dict:
    arg_keys = jax.random.split(jax.random.key(seed), 7)
    bin_codes = touch_ends(jax.random.randint(arg_keys[0], (TOTAL_ROWS, FEATURES), 0, BINS), jax.random.fold_in(arg_keys[0], 1), 0, BINS - 1).astype(jnp.int32)
    leaf_index_keys = jax.random.split(jax.random.fold_in(arg_keys[1], 1), TOTAL_ROWS // ROW_DEV)
    leaf_index_turns = jax.random.permutation(jax.random.fold_in(arg_keys[1], 3), TOTAL_ROWS // ROW_DEV)
    leaf_index = jax.vmap(lambda own, number: assign_block(jax.random.fold_in(arg_keys[1], 2), own, number, ROW_DEV, LEAVES, 1, CAP, 2))(leaf_index_keys, leaf_index_turns).reshape((TOTAL_ROWS, 1))
    gradients = bell_draw(arg_keys[2], (TOTAL_ROWS, TARGETS), 1.0, 6.0, ((0, 32),))
    row_weights = jnp.clip(jnp.exp(math.log(2.0) - 1.3862944 * jax.random.uniform(arg_keys[3], (TOTAL_ROWS,), jnp.float32) ** levels(arg_keys[3], (TOTAL_ROWS,), ((0, 32),), -0.2, 0.2)), 0.5, 2.0).astype(jnp.bfloat16)
    split_feature = jax.random.randint(arg_keys[4], (1,), 0, FEATURES).astype(jnp.int32)
    split_bin = jax.random.randint(arg_keys[5], (1,), 0, BINS - 1).astype(jnp.int32)
    return {"bin_codes": bin_codes, "leaf_index": leaf_index, "gradients": gradients, "row_weights": row_weights, "split_feature": split_feature, "split_bin": split_bin}


ridge = 1.0


def split_scores(grad_hist, weight_hist):
    left_g = jnp.cumsum(grad_hist, axis=1)
    left_w = jnp.cumsum(weight_hist, axis=1)
    upper_g = jnp.flip(jnp.cumsum(jnp.flip(grad_hist, axis=1), axis=1), axis=1)
    upper_w = jnp.flip(jnp.cumsum(jnp.flip(weight_hist, axis=1), axis=1), axis=1)
    right_g = jnp.concatenate([upper_g[:, 1:], jnp.zeros_like(upper_g[:, :1])], axis=1)
    right_w = jnp.concatenate([upper_w[:, 1:], jnp.zeros_like(upper_w[:, :1])], axis=1)
    left_x = left_w + ridge
    right_y = right_w + ridge
    diff = left_g * right_y[..., None] - right_g * left_x[..., None]
    terms = diff * diff / (left_x * right_y * (left_x + right_y))[..., None]
    return jnp.sum(terms, axis=(2, 3)) / (LEAVES * TARGETS)


def place_rows(leaf, child, grads, weights):
    key_ids = leaf * 2 + child
    key_hot = (key_ids[:, None] == jnp.arange(2 * LEAVES, dtype=jnp.int32)[None, :]).astype(jnp.int32)
    before = jnp.cumsum(key_hot, axis=0) - key_hot
    rank = jnp.sum(before * key_hot, axis=1)
    counts = jnp.sum(key_hot, axis=0)
    leaf_hot = (leaf[:, None] == jnp.arange(LEAVES, dtype=jnp.int32)[None, :]).astype(jnp.int32)
    first = jnp.sum(leaf_hot * counts[0::2][None, :], axis=1)
    slot = (leaf * CAP + rank + child * first).astype(jnp.int32)
    buf_g = jnp.zeros((LEAVES * CAP, grads.shape[1]), grads.dtype).at[slot].set(grads)
    buf_w = jnp.zeros((LEAVES * CAP,), weights.dtype).at[slot].set(weights)
    return buf_g.reshape(LEAVES, CAP * grads.shape[1]), buf_w.reshape(LEAVES, CAP)


def reference(bin_codes, leaf_index, gradients, row_weights, split_feature, split_bin):
    leaf = leaf_index[:, 0]
    data = jnp.concatenate([gradients.astype(jnp.float32), row_weights.astype(jnp.float32)[:, None]], axis=1)

    def one_feature(index):
        column = lax.dynamic_slice_in_dim(bin_codes, index, 1, 1)[:, 0]
        return jax.ops.segment_sum(data, column * LEAVES + leaf, num_segments=BINS * LEAVES)

    hist = lax.map(one_feature, jnp.arange(FEATURES, dtype=jnp.int32))
    hist = hist.reshape(FEATURES, BINS, LEAVES, TARGETS + 1)
    gain_table = split_scores(hist[..., :TARGETS], hist[..., TARGETS]).reshape(FEATURES * BINS)
    best_gain = jnp.max(gain_table).reshape(1)
    column = lax.dynamic_slice_in_dim(bin_codes, split_feature[0].astype(jnp.int32), 1, 1)[:, 0]
    child = (column > split_bin[0]).astype(jnp.int32)
    blocks = N_ROWS * N_GRP
    buf_g, buf_w = jax.vmap(place_rows)(leaf.reshape(blocks, ROW_DEV), child.reshape(blocks, ROW_DEV),
                                        gradients.reshape(blocks, ROW_DEV, TARGETS), row_weights.reshape(blocks, ROW_DEV))
    moved_gradients = buf_g.reshape(N_ROWS, N_GRP, LEAVES, CAP * TARGETS).transpose(0, 2, 1, 3).reshape(N_ROWS * LEAVES, N_GRP * CAP * TARGETS)
    moved_weights = buf_w.reshape(N_ROWS, N_GRP, LEAVES, CAP).transpose(0, 2, 1, 3).reshape(N_ROWS * LEAVES, N_GRP * CAP)
    return gain_table, best_gain, moved_gradients, moved_weights
```

```python
import functools

import jax
import jax.numpy as jnp
from jax import lax
from jax.experimental import pallas as pl
from jax.experimental.pallas import tpu as pltpu
from jax.sharding import PartitionSpec as P

BINS = 32
TARGETS = 16
LEAVES = 8
CAP = 1024
LANES = 128
CHUNKS = 4
ridge = 1.0
VMEM_LIMIT = 56 * 1024 * 1024
NT = (((1,), (1,)), ((), ()))


def params(**kw):
    return pltpu.CompilerParams(vmem_limit_bytes=VMEM_LIMIT, **kw)


def prep_kernel(feat_ref, codes_ref, leaf_ref, grad_ref, weight_ref, turned_ref, column_ref, data_ref):
    turned = codes_ref[...].astype(jnp.float32).T.astype(jnp.bfloat16)
    turned_ref[...] = turned
    features = turned.shape[0]
    pick = lax.broadcasted_iota(jnp.int32, (8, features), 1) == feat_ref[0]
    pick = jnp.where(pick, 1.0, 0.0).astype(jnp.bfloat16)
    column_ref[...] = jnp.dot(pick, turned, preferred_element_type=jnp.float32)
    leaf = leaf_ref[...]
    step = leaf.shape[1]
    grads = grad_ref[...].astype(jnp.float32)
    parts = [jnp.where(leaf == l, grads, 0.0) for l in range(LEAVES)]
    ids = lax.broadcasted_iota(jnp.int32, (LANES, step), 0)
    parts.append(jnp.where(ids == leaf, weight_ref[...].astype(jnp.float32), 0.0))
    data_ref[...] = jnp.concatenate(parts, axis=0).T.astype(jnp.bfloat16)


def partition_kernel(bin_ref, leaf_ref, column_ref, grad_ref, weight_ref, out_g_ref, out_w_ref):
    keys = 2 * LEAVES
    rows = leaf_ref.shape[1]
    leaf = leaf_ref[...]
    child = jnp.where(column_ref[0:1, :] > bin_ref[0].astype(jnp.float32), 1, 0)
    key = leaf * 2 + child
    hot = jnp.where(lax.broadcasted_iota(jnp.int32, (keys, rows), 0) == key, 1.0, 0.0)
    counts = jnp.sum(hot, axis=1, keepdims=True)
    key_ids = lax.broadcasted_iota(jnp.int32, (keys, 1), 0)
    base = jnp.where(key_ids % 2 == 1, pltpu.roll(jnp.broadcast_to(counts, (keys, LANES)), 1, 0)[:, 0:1], 0.0)
    base = base + (key_ids // 2 * CAP).astype(jnp.float32)
    width = 256
    upper = jnp.where(
        lax.broadcasted_iota(jnp.int32, (width, width), 0)
        < lax.broadcasted_iota(jnp.int32, (width, width), 1),
        1.0,
        0.0,
    ).astype(jnp.bfloat16)
    slots = []
    for c in range(rows // width):
        part = hot[:, c * width : (c + 1) * width]
        rank = jnp.dot(part.astype(jnp.bfloat16), upper, preferred_element_type=jnp.float32)
        slots.append(jnp.sum(part * (rank + base), axis=0, keepdims=True))
        base = base + jnp.sum(part, axis=1, keepdims=True)
    per = LANES // TARGETS
    group = LEAVES * CAP // per
    pages = LEAVES * CAP // LANES
    wide = 512
    acc_g = jnp.zeros((group, LANES), jnp.float32)
    acc_w = jnp.zeros((pages, LANES), jnp.float32)
    for c in range(rows // wide):
        many = wide // width
        slot = jnp.concatenate(slots[c * many : (c + 1) * many], axis=1).astype(jnp.int32)
        span = slice(c * wide, (c + 1) * wide)
        grads = grad_ref[:, span].astype(jnp.float32)
        lhs = jnp.where(
            lax.broadcasted_iota(jnp.int32, (group, wide), 0) == slot // per, 1.0, 0.0
        ).astype(jnp.bfloat16)
        rest = slot % per
        rhs = jnp.concatenate([jnp.where(rest == k, grads, 0.0) for k in range(per)], axis=0)
        acc_g += lax.dot_general(lhs, rhs.astype(jnp.bfloat16), NT, preferred_element_type=jnp.float32)
        lhs = jnp.where(
            lax.broadcasted_iota(jnp.int32, (pages, wide), 0) == slot // LANES, 1.0, 0.0
        ).astype(jnp.bfloat16)
        rhs = jnp.where(
            lax.broadcasted_iota(jnp.int32, (LANES, wide), 0) == slot % LANES,
            weight_ref[:, span].astype(jnp.float32),
            0.0,
        ).astype(jnp.bfloat16)
        acc_w += lax.dot_general(lhs, rhs, NT, preferred_element_type=jnp.float32)
    out_g_ref[...] = acc_g.astype(jnp.bfloat16)
    out_w_ref[...] = acc_w.astype(jnp.bfloat16)


def hist_kernel(first, count, owners, turned_ref, data_ref, out_ref, w_ref):
    features = turned_ref.shape[0]
    own = features // owners
    w_ref[...] = jnp.zeros_like(w_ref)

    def one_bin(b, carry):
        which = (first + b).astype(jnp.float32).astype(jnp.bfloat16)
        hot = jnp.where(turned_ref[...] == which, 1.0, 0.0).astype(jnp.bfloat16)
        both = jnp.dot(hot, data_ref[...], preferred_element_type=jnp.float32)
        for d in range(owners):
            out_ref[d, b] = both[d * own : (d + 1) * own, :LANES]
        w_ref[...] += pltpu.roll(both[:, LANES:], b * LEAVES, 1)
        return carry

    lax.fori_loop(0, count, one_bin, 0)
    for d in range(owners):
        out_ref[d, count] = w_ref[d * own : (d + 1) * own, :]


def gain_kernel(count, *refs):
    parts, out_ref = refs[:-1], refs[-1]
    own = out_ref.shape[0]
    left_g, left_w = [], []
    row = lax.broadcasted_iota(jnp.int32, (LANES, LANES), 0)
    col = lax.broadcasted_iota(jnp.int32, (LANES, LANES), 1)
    grad_hist, weight_hist = [], []
    for part in parts:
        weights = part[count]
        for b in range(count):
            spread = jnp.where(row == b * LEAVES + col // TARGETS, 1.0, 0.0)
            grad_hist.append(part[b])
            weight_hist.append(
                jnp.dot(weights, spread, precision=lax.Precision.HIGHEST, preferred_element_type=jnp.float32)
            )
    bins = len(grad_hist)
    right_g = [jnp.zeros_like(grad_hist[0])] * bins
    right_w = [jnp.zeros_like(weight_hist[0])] * bins
    for b in range(bins - 2, -1, -1):
        right_g[b] = right_g[b + 1] + grad_hist[b + 1]
        right_w[b] = right_w[b + 1] + weight_hist[b + 1]
    lane = lax.broadcasted_iota(jnp.int32, (own, LANES), 1)
    table = jnp.zeros((own, LANES), jnp.float32)
    left_g = jnp.zeros_like(grad_hist[0])
    left_w = jnp.zeros_like(weight_hist[0])
    for b in range(bins):
        left_g = left_g + grad_hist[b]
        left_w = left_w + weight_hist[b]
        x = left_w + ridge
        y = right_w[b] + ridge
        diff = left_g * y - right_g[b] * x
        terms = diff * diff / (x * y * (x + y))
        score = jnp.sum(terms, axis=1, keepdims=True) / (LEAVES * TARGETS)
        table = jnp.where(lane == b, score, table)
    out_ref[...] = table


def shards(owners, bin_codes, leaf_index, gradients, row_weights, split_feature, split_bin):
    rows, features = bin_codes.shape
    leaf = leaf_index.T
    grads = gradients.T
    weights = row_weights.reshape(1, rows)
    step = 512
    vm = pl.BlockSpec(memory_space=pltpu.VMEM)
    sm = pl.BlockSpec(memory_space=pltpu.SMEM)
    turned, column, data = pl.pallas_call(
        prep_kernel,
        grid=(rows // step,),
        in_specs=[
            sm,
            pl.BlockSpec((step, features), lambda i: (i, 0)),
            pl.BlockSpec((1, step), lambda i: (0, i)),
            pl.BlockSpec((TARGETS, step), lambda i: (0, i)),
            pl.BlockSpec((1, step), lambda i: (0, i)),
        ],
        out_specs=[
            pl.BlockSpec((features, step), lambda i: (0, i)),
            pl.BlockSpec((8, step), lambda i: (0, i)),
            pl.BlockSpec((step, 2 * LANES), lambda i: (i, 0)),
        ],
        out_shape=[
            jax.ShapeDtypeStruct((features, rows), jnp.bfloat16),
            jax.ShapeDtypeStruct((8, rows), jnp.float32),
            jax.ShapeDtypeStruct((rows, 2 * LANES), jnp.bfloat16),
        ],
        compiler_params=params(),
        name="prep",
    )(split_feature, bin_codes, leaf, grads, weights)

    per = LANES // TARGETS
    send_g, send_w = pl.pallas_call(
        partition_kernel,
        in_specs=[sm, vm, vm, vm, vm],
        out_specs=[vm, vm],
        out_shape=[
            jax.ShapeDtypeStruct((LEAVES * CAP // per, LANES), jnp.bfloat16),
            jax.ShapeDtypeStruct((LEAVES * CAP // LANES, LANES), jnp.bfloat16),
        ],
        compiler_params=params(),
        name="partition",
    )(split_bin, leaf, column, grads, weights)
    send_g = send_g.reshape(LEAVES, CAP * TARGETS)
    send_w = send_w.reshape(LEAVES, CAP)
    moved_gradients = lax.all_to_all(send_g, "grp", split_axis=0, concat_axis=1, tiled=True)
    moved_weights = lax.all_to_all(send_w, "grp", split_axis=0, concat_axis=1, tiled=True)

    count = BINS // CHUNKS
    own = features // owners
    parts = []
    for c in range(CHUNKS):
        term = pl.pallas_call(
            functools.partial(hist_kernel, c * count, count, owners),
            in_specs=[vm, vm],
            out_specs=vm,
            out_shape=jax.ShapeDtypeStruct((owners, count + 1, own, LANES), jnp.float32),
            scratch_shapes=[pltpu.VMEM((features, LANES), jnp.float32)],
            compiler_params=params(),
            cost_estimate=pl.CostEstimate(
                flops=4 * features * count * rows * LANES, bytes_accessed=8 << 20, transcendentals=0
            ),
            name="hist",
        )(turned, data)
        parts.append(
            lax.psum_scatter(term, ("rows", "grp"), scatter_dimension=0, tiled=True).reshape(
                count + 1, own, LANES
            )
        )
    table = pl.pallas_call(
        functools.partial(gain_kernel, count),
        in_specs=[vm] * CHUNKS,
        out_specs=vm,
        out_shape=jax.ShapeDtypeStruct((own, LANES), jnp.float32),
        compiler_params=params(),
        name="gain",
    )(*parts)
    gain_local = table[:, :BINS].reshape(-1)
    everything = lax.all_gather(gain_local, ("rows", "grp"), axis=0, tiled=True)
    best_gain = jnp.max(everything).reshape(1)
    share = everything.shape[0] // lax.axis_size("rows")
    gain_table = lax.dynamic_slice_in_dim(everything, lax.axis_index("rows") * share, share, 0)
    return (gain_table, best_gain, moved_gradients, moved_weights)


def solution(mesh):
    placed = (
        P(("rows", "grp"), None),
        P(("rows", "grp"), None),
        P(("rows", "grp"), None),
        P(("rows", "grp")),
        P(),
        P(),
    )
    return jax.shard_map(
        functools.partial(shards, mesh.shape["rows"] * mesh.shape["grp"]),
        mesh=mesh,
        in_specs=placed,
        out_specs=(P("rows"), P(), P(("rows", "grp"), None), P(("rows", "grp"), None)),
        check_vma=False,
    )
```
